32 devices in a mesh: dp: 16 (over z, y, core), tensor: 2 (over x).
Axes of the slice: x: 2, y: 2, z: 4, core: 2. Of those that a mesh axis runs over, the one named last changes fastest.
Arguments:
- block_input: bfloat16 [16384, 1536], P('dp'), may hold values from -50 to 50
- cotangent: bfloat16 [16384, 1536], P('dp'), may hold values from -6 to 6
- pre_gain: float32 [1536], replicated, may hold values from 0.5 to 1.5
- gate_proj: bfloat16 [1536, 3072], P(None, 'tensor'), may hold values from -0.15625 to 0.15625
- value_proj: bfloat16 [1536, 3072], P(None, 'tensor'), may hold values from -0.15625 to 0.15625
- step_proj: bfloat16 [1536, 48], P(None, 'tensor'), may hold values from -0.15625 to 0.15625
- state_proj: bfloat16 [1536, 256], replicated, may hold values from -0.15625 to 0.15625
- conv_value: float32 [4, 3072], P(None, 'tensor'), may hold values from -3 to 3
- conv_value_bias: float32 [3072], P('tensor'), may hold values from -3 to 3
- conv_state: float32 [4, 256], replicated, may hold values from -3 to 3
- conv_state_bias: float32 [256], replicated, may hold values from -3 to 3
- step_bias: float32 [48], P('tensor'), may hold values from -6.9 to -2.3
- decay_log: float32 [48], P('tensor'), may hold values from 0 to 2.77
- skip_gain: float32 [48], P('tensor'), may hold values from 0.5 to 1.5
- norm_gain: float32 [3072], P('tensor'), may hold values from 0.5 to 1.5
- out_proj: bfloat16 [3072, 1536], P('tensor'), may hold values from -0.109375 to 0.109375
Outputs:
- block_out: bfloat16 [16384, 1536], P('dp')
- grad_input: float32 [16384, 1536], P('dp')
- grad_pre_gain: float32 [1536], replicated
- grad_gate_proj: float32 [1536, 3072], P(None, 'tensor')
- grad_value_proj: float32 [1536, 3072], P(None, 'tensor')
- grad_step_proj: float32 [1536, 48], P(None, 'tensor')
- grad_state_proj: float32 [1536, 256], replicated
- grad_conv_value: float32 [4, 3072], P(None, 'tensor')
- grad_conv_value_bias: float32 [3072], P('tensor')
- grad_conv_state: float32 [4, 256], replicated
- grad_conv_state_bias: float32 [256], replicated
- grad_step_bias: float32 [48], P('tensor')
- grad_decay_log: float32 [48], P('tensor')
- grad_skip_gain: float32 [48], P('tensor')
- grad_norm_gain: float32 [3072], P('tensor')
- grad_out_proj: float32 [3072, 1536], P('tensor')
The draws below stay inside these ranges and needn't reach their ends.
All inputs are finite; a program needn't handle non-finite values.
Results may differ from the reference program's by a relative error of at most 0.008.
Values may be sent and summed in bfloat16 or wider, within the bound.
No kernel may reach another device: no remote copies, remote signals or barrier semaphores. Data moves between devices by JAX's collectives and lax.ppermute only.
A program may use at most 256 MiB of HBM per device.

```python
import jax
import jax.numpy as jnp
from jax import lax

D = 1536
HEADS = 48
STATE = 128
KERNEL = 4
BLOCK = 256
SEQ_LEN = 1024
INNER = 3072
TOKENS = 16384


def draw_block_input(key, part):
    row_key, column_key, base_key = jax.random.split(key, 3)
    row_scale = jnp.exp(jax.random.uniform(row_key, (TOKENS, 1), jnp.float32, -1.15, 1.15))
    column_scale = jnp.exp(jax.random.uniform(column_key, (1, D), jnp.float32, -1.15, 1.15))
    base = jnp.clip(jax.random.normal(base_key, (TOKENS, D), jnp.float32), -5.0, 5.0)
    return (base * row_scale * column_scale).astype(jnp.bfloat16)


def shard_levels(stream_key, extent, pieces, least, top_value):
    loudness = 1.0
    for position, parts in pieces:
        steps = jax.random.uniform(jax.random.fold_in(jax.random.fold_in(stream_key, 6), position), (parts,), jnp.float32, least / len(pieces), top_value / len(pieces))
        loudness = loudness * jnp.repeat(jnp.exp(steps), extent[position] // parts).reshape((-1,) + (1,) * (len(extent) - 1 - position))
    return loudness


def scatter_about(rng, dims, deviation, limit, shards=(), dtype=jnp.bfloat16):
    values = jax.random.normal(rng, dims, jnp.float32) * deviation
    if len(shards) > 0:
        values = shard_levels(rng, dims, shards, -0.22, 0.18) * values
    return jnp.clip(values, min=-limit, max=limit).astype(dtype)


def setup_inputs(seed: int = 0) -> dict:
    arg_keys = jax.random.split(jax.random.key(seed), 17)
    block_input = draw_block_input(jax.random.fold_in(arg_keys[16], 71), 0)
    cotangent = scatter_about(arg_keys[1], (TOKENS, D), 1.0, 6.0, ((0, 16),))
    pre_gain = jnp.clip(1.0 + 0.1 * jax.random.normal(arg_keys[2], (D,), jnp.float32), 0.5, 1.5)
    gate_proj = scatter_about(arg_keys[3], (D, INNER), D ** -0.5, 0.15625, ((1, 2),))
    value_proj = scatter_about(arg_keys[4], (D, INNER), D ** -0.5, 0.15625, ((1, 2),))
    step_proj = scatter_about(arg_keys[5], (D, HEADS), D ** -0.5, 0.15625, ((1, 2),))
    state_proj = scatter_about(arg_keys[6], (D, 2 * STATE), D ** -0.5, 0.15625)
    conv_value = scatter_about(arg_keys[7], (KERNEL, INNER), KERNEL ** -0.5, 3.0, ((1, 2),), jnp.float32)
    conv_value_bias = scatter_about(arg_keys[8], (INNER,), 0.5, 3.0, ((0, 2),), jnp.float32)
    conv_state = scatter_about(arg_keys[9], (KERNEL, 2 * STATE), KERNEL ** -0.5, 3.0, (), jnp.float32)
    conv_state_bias = scatter_about(arg_keys[10], (2 * STATE,), 0.5, 3.0, (), jnp.float32)
    step_bias = jnp.clip(-6.9 + 4.6000001430511475 * jax.random.uniform(arg_keys[11], (HEADS,), jnp.float32) ** shard_levels(arg_keys[11], (HEADS,), ((0, 2),), -0.2, 0.2), -6.9, -2.3)
    decay_log = jnp.clip(2.77 * jax.random.uniform(arg_keys[12], (HEADS,), jnp.float32) ** shard_levels(arg_keys[12], (HEADS,), ((0, 2),), -0.2, 0.2), 0.0, 2.77)
    skip_gain = jnp.clip(0.5 + 1.0 * jax.random.uniform(arg_keys[13], (HEADS,), jnp.float32) ** shard_levels(arg_keys[13], (HEADS,), ((0, 2),), -0.2, 0.2), 0.5, 1.5)
    norm_gain = jnp.clip(1.0 + 0.1 * jax.random.normal(arg_keys[14], (INNER,), jnp.float32), 0.5, 1.5)
    out_proj = scatter_about(arg_keys[15], (INNER, D), INNER ** -0.5, 0.109375, ((0, 2),))
    return {"block_input": block_input, "cotangent": cotangent, "pre_gain": pre_gain, "gate_proj": gate_proj, "value_proj": value_proj, "step_proj": step_proj, "state_proj": state_proj, "conv_value": conv_value, "conv_value_bias": conv_value_bias, "conv_state": conv_state, "conv_state_bias": conv_state_bias, "step_bias": step_bias, "decay_log": decay_log, "skip_gain": skip_gain, "norm_gain": norm_gain, "out_proj": out_proj}


epsilon = 1e-05
highest = lax.Precision.HIGHEST

def causal_conv(values, kernel, offset):
    kernel_width = kernel.shape[0]
    length = values.shape[0]
    padded = jnp.concatenate([jnp.zeros((kernel_width - 1, values.shape[1]), jnp.float32), values], axis=0)
    running_sum = jnp.zeros_like(values) + offset[None, :]
    for tap_index in range(kernel_width):
        running_sum = running_sum + kernel[tap_index][None, :] * padded[tap_index:tap_index + length]
    return running_sum

def make_states(bc_raw, conv_state, conv_state_bias):
    return jax.nn.silu(causal_conv(bc_raw, conv_state, conv_state_bias))

def mixer(conv_in, states, step_raw, gate_raw, conv_value, conv_value_bias, step_bias, decay_log, skip_gain):
    length = conv_in.shape[0]
    head_count = skip_gain.shape[0]
    head_width = conv_in.shape[1] // head_count
    state_width = states.shape[1] // 2
    block_count = length // BLOCK
    conv_out = jax.nn.silu(causal_conv(conv_in, conv_value, conv_value_bias))
    step_size = jax.nn.softplus(step_raw + step_bias[None, :])
    decay_rate = -jnp.exp(decay_log)
    log_decay = step_size * decay_rate[None, :]
    writer = states[:, :state_width].reshape(block_count, BLOCK, state_width)
    reader = states[:, state_width:].reshape(block_count, BLOCK, state_width)
    head_values = conv_out.reshape(block_count, BLOCK, head_count, head_width)
    cumulative = jnp.cumsum(log_decay.reshape(block_count, BLOCK, head_count), axis=1)
    cum_heads = jnp.transpose(cumulative, (0, 2, 1))
    step_heads = jnp.transpose(step_size.reshape(block_count, BLOCK, head_count), (0, 2, 1))
    scores = jnp.einsum('ktn,ksn->kts', reader, writer, precision=highest)
    causal_mask = jnp.tril(jnp.ones((BLOCK, BLOCK), jnp.float32))
    log_gap = cum_heads[:, :, :, None] - cum_heads[:, :, None, :]
    decay = jnp.exp(jnp.where(causal_mask > 0, log_gap, 0.0)) * causal_mask
    weights = scores[:, None, :, :] * decay * step_heads[:, :, None, :]
    intra_part = jnp.einsum('khts,kshp->kthp', weights, head_values, precision=highest)
    tail_weight = jnp.exp(cum_heads[:, :, -1:] - cum_heads) * step_heads
    block_state = jnp.einsum('ksn,khs,kshp->khnp', writer, tail_weight, head_values, precision=highest)
    block_fade = jnp.exp(cum_heads[:, :, -1])

    def advance(carried, item):
        new_part, keep_factor = item
        return (carried * keep_factor[:, None, None] + new_part, carried)
    initial = jnp.zeros((head_count, state_width, head_width), jnp.float32)
    _, entering = lax.scan(advance, initial, (block_state, block_fade))
    inter_part = jnp.einsum('ktn,khnp->kthp', reader, entering, precision=highest) * jnp.exp(cumulative)[:, :, :, None]
    mixed_out = intra_part + inter_part + skip_gain[None, None, :, None] * head_values
    mixed_out = mixed_out.reshape(length, head_count * head_width)
    return mixed_out * jax.nn.silu(gate_raw)

def dot_plain(left, right):
    return jnp.dot(left, right, preferred_element_type=jnp.float32)

def dot_inner(left, right):
    return lax.dot_general(left, right, (((0,), (0,)), ((), ())), preferred_element_type=jnp.float32)

def dot_outer(left, right):
    return lax.dot_general(left, right, (((1,), (1,)), ((), ())), preferred_element_type=jnp.float32)

def reference(block_input, cotangent, pre_gain, gate_proj, value_proj, step_proj, state_proj, conv_value, conv_value_bias, conv_state, conv_state_bias, step_bias, decay_log, skip_gain, norm_gain, out_proj):
    seq_count = block_input.shape[0] // SEQ_LEN
    seq_inputs = block_input.reshape(seq_count, SEQ_LEN, D)
    seq_cotangents = cotangent.reshape(seq_count, SEQ_LEN, D)
    params = (pre_gain, gate_proj, value_proj, step_proj, state_proj, conv_value, conv_value_bias, conv_state, conv_state_bias, step_bias, decay_log, skip_gain, norm_gain, out_proj)
    zero_sums = jax.tree.map(lambda weight: jnp.zeros(weight.shape, jnp.float32), params)

    def one_sequence(sums, item):
        rows_in, rows_cot = item
        input_f32 = rows_in.astype(jnp.float32)
        pre_scale = lax.rsqrt(lax.optimization_barrier(jnp.mean(input_f32 * input_f32, axis=1, keepdims=True)) + epsilon)
        normed = (input_f32 * pre_scale * pre_gain[None, :]).astype(jnp.bfloat16)
        gate_raw = dot_plain(normed, gate_proj)
        conv_in = dot_plain(normed, value_proj)
        step_raw = dot_plain(normed, step_proj)
        bc_raw = dot_plain(normed, state_proj)
        states, state_back = jax.vjp(make_states, bc_raw, conv_state, conv_state_bias)
        gated, mixer_back = jax.vjp(mixer, conv_in, states, step_raw, gate_raw, conv_value, conv_value_bias, step_bias, decay_log, skip_gain)
        gate_scale = lax.rsqrt(lax.optimization_barrier(jnp.mean(gated * gated, axis=1, keepdims=True)) + epsilon)
        gated_normed = (gated * gate_scale * norm_gain[None, :]).astype(jnp.bfloat16)
        block_out = (input_f32 + dot_plain(gated_normed, out_proj)).astype(jnp.bfloat16)
        d_gn = dot_outer(rows_cot, out_proj)
        grad_out_proj = dot_inner(gated_normed, rows_cot)
        grad_norm_gain = lax.optimization_barrier(jnp.sum(d_gn * gated * gate_scale, axis=0))
        gate_dot = lax.optimization_barrier(jnp.sum(d_gn * norm_gain[None, :] * gated, axis=1, keepdims=True))
        d_gated = gate_scale * norm_gain[None, :] * d_gn - gated * gate_scale ** 3 * gate_dot / INNER
        d_conv_in, d_states, d_step_raw, d_gate_raw, grad_conv_value, grad_conv_value_bias, grad_step_bias, grad_decay_log, grad_skip_gain = mixer_back(d_gated)
        d_bc_raw, grad_conv_state, grad_conv_state_bias = state_back(d_states)
        gate_bf = d_gate_raw.astype(jnp.bfloat16)
        value_bf = d_conv_in.astype(jnp.bfloat16)
        step_bf = d_step_raw.astype(jnp.bfloat16)
        state_bf = d_bc_raw.astype(jnp.bfloat16)
        d_normed = dot_outer(gate_bf, gate_proj) + dot_outer(value_bf, value_proj) + dot_outer(step_bf, step_proj) + dot_outer(state_bf, state_proj)
        grad_pre_gain = lax.optimization_barrier(jnp.sum(d_normed * input_f32 * pre_scale, axis=0))
        pre_dot = lax.optimization_barrier(jnp.sum(d_normed * pre_gain[None, :] * input_f32, axis=1, keepdims=True))
        grad_rows = rows_cot.astype(jnp.float32) + pre_scale * pre_gain[None, :] * d_normed - input_f32 * pre_scale ** 3 * pre_dot / D
        terms = (grad_pre_gain, dot_inner(normed, gate_bf), dot_inner(normed, value_bf), dot_inner(normed, step_bf), dot_inner(normed, state_bf), grad_conv_value, grad_conv_value_bias, grad_conv_state, grad_conv_state_bias, grad_step_bias, grad_decay_log, grad_skip_gain, grad_norm_gain, grad_out_proj)
        sums = jax.tree.map(lambda accumulated, addition: accumulated + addition, sums, terms)
        return (sums, (block_out, grad_rows))
    totals, (outputs, gradients) = lax.scan(one_sequence, zero_sums, (seq_inputs, seq_cotangents))
    block_out = outputs.reshape(block_input.shape[0], D)
    grad_input = gradients.reshape(block_input.shape[0], D)
    return (block_out, grad_input, totals[0], totals[1], totals[2], totals[3], totals[4], totals[5], totals[6], totals[7], totals[8], totals[9], totals[10], totals[11], totals[12], totals[13])
```

```python
import jax
import jax.numpy as jnp
from jax import lax
from jax.sharding import PartitionSpec as P

D = 1536
BLOCK = 256
SEQ_LEN = 1024
INNER = 3072


epsilon = 1e-05
highest = lax.Precision.HIGHEST


def causal_conv(values, kernel, offset):
    kernel_width = kernel.shape[0]
    length = values.shape[0]
    padded = jnp.concatenate(
        [jnp.zeros((kernel_width - 1, values.shape[1]), jnp.float32), values], axis=0
    )
    running_sum = jnp.zeros_like(values) + offset[None, :]
    for tap_index in range(kernel_width):
        running_sum = (
            running_sum + kernel[tap_index][None, :] * padded[tap_index : tap_index + length]
        )
    return running_sum


def make_states(bc_raw, conv_state, conv_state_bias):
    return jax.nn.silu(causal_conv(bc_raw, conv_state, conv_state_bias))


def mixer(
    conv_in,
    states,
    step_raw,
    gate_raw,
    conv_value,
    conv_value_bias,
    step_bias,
    decay_log,
    skip_gain,
):
    length = conv_in.shape[0]
    head_count = skip_gain.shape[0]
    head_width = conv_in.shape[1] // head_count
    state_width = states.shape[1] // 2
    block_count = length // BLOCK
    conv_out = jax.nn.silu(causal_conv(conv_in, conv_value, conv_value_bias))
    step_size = jax.nn.softplus(step_raw + step_bias[None, :])
    decay_rate = -jnp.exp(decay_log)
    log_decay = step_size * decay_rate[None, :]
    writer = states[:, :state_width].reshape(block_count, BLOCK, state_width)
    reader = states[:, state_width:].reshape(block_count, BLOCK, state_width)
    head_values = conv_out.reshape(block_count, BLOCK, head_count, head_width)
    cumulative = jnp.cumsum(log_decay.reshape(block_count, BLOCK, head_count), axis=1)
    cum_heads = jnp.transpose(cumulative, (0, 2, 1))
    step_heads = jnp.transpose(step_size.reshape(block_count, BLOCK, head_count), (0, 2, 1))
    scores = jnp.einsum("ktn,ksn->kts", reader, writer, precision=highest)
    causal_mask = jnp.tril(jnp.ones((BLOCK, BLOCK), jnp.float32))
    log_gap = cum_heads[:, :, :, None] - cum_heads[:, :, None, :]
    decay = jnp.exp(jnp.where(causal_mask > 0, log_gap, 0.0)) * causal_mask
    weights = scores[:, None, :, :] * decay * step_heads[:, :, None, :]
    intra_part = jnp.einsum("khts,kshp->kthp", weights, head_values, precision=highest)
    tail_weight = jnp.exp(cum_heads[:, :, -1:] - cum_heads) * step_heads
    block_state = jnp.einsum(
        "ksn,khs,kshp->khnp", writer, tail_weight, head_values, precision=highest
    )
    block_fade = jnp.exp(cum_heads[:, :, -1])

    def advance(carried, item):
        new_part, keep_factor = item
        return (carried * keep_factor[:, None, None] + new_part, carried)

    initial = jnp.zeros((head_count, state_width, head_width), jnp.float32)
    _, entering = lax.scan(advance, initial, (block_state, block_fade))
    inter_part = (
        jnp.einsum("ktn,khnp->kthp", reader, entering, precision=highest)
        * jnp.exp(cumulative)[:, :, :, None]
    )
    mixed_out = intra_part + inter_part + skip_gain[None, None, :, None] * head_values
    mixed_out = mixed_out.reshape(length, head_count * head_width)
    return mixed_out * jax.nn.silu(gate_raw)


def dot_plain(left, right):
    return jnp.dot(left, right, preferred_element_type=jnp.float32)


def dot_inner(left, right):
    return lax.dot_general(
        left, right, (((0,), (0,)), ((), ())), preferred_element_type=jnp.float32
    )


def dot_outer(left, right):
    return lax.dot_general(
        left, right, (((1,), (1,)), ((), ())), preferred_element_type=jnp.float32
    )


def local(
    block_input,
    cotangent,
    pre_gain,
    gate_proj,
    value_proj,
    step_proj,
    state_proj,
    conv_value,
    conv_value_bias,
    conv_state,
    conv_state_bias,
    step_bias,
    decay_log,
    skip_gain,
    norm_gain,
    out_proj,
):
    row_count = block_input.shape[0]
    seq_count = row_count // SEQ_LEN

    def by_sequence(array):
        return array.reshape(seq_count, SEQ_LEN, array.shape[1])

    def by_row(array):
        return array.reshape(row_count, array.shape[2])

    input_f32 = block_input.astype(jnp.float32)
    pre_scale = lax.rsqrt(jnp.mean(input_f32 * input_f32, axis=1, keepdims=True) + epsilon)
    normed = (input_f32 * pre_scale * pre_gain[None, :]).astype(jnp.bfloat16)
    gate_raw = dot_plain(normed, gate_proj)
    conv_in = dot_plain(normed, value_proj)
    step_raw = dot_plain(normed, step_proj)
    bc_raw = dot_plain(normed, state_proj)
    states, state_back = jax.vjp(
        jax.vmap(make_states, in_axes=(0, None, None)),
        by_sequence(bc_raw),
        conv_state,
        conv_state_bias,
    )
    gated_seq, mixer_back = jax.vjp(
        jax.vmap(mixer, in_axes=(0, 0, 0, 0, None, None, None, None, None)),
        by_sequence(conv_in),
        states,
        by_sequence(step_raw),
        by_sequence(gate_raw),
        conv_value,
        conv_value_bias,
        step_bias,
        decay_log,
        skip_gain,
    )
    gated = by_row(gated_seq)
    d_gn = dot_outer(cotangent, out_proj)
    weighted = d_gn * norm_gain[None, :]
    row_sums = lax.psum(
        jnp.stack([jnp.sum(gated * gated, axis=1), jnp.sum(weighted * gated, axis=1)]), "tensor"
    )
    gate_scale = lax.rsqrt(row_sums[0][:, None] / INNER + epsilon)
    gate_dot = row_sums[1][:, None]
    gated_normed = (gated * gate_scale * norm_gain[None, :]).astype(jnp.bfloat16)
    swap = [(0, 1), (1, 0)]
    branch = dot_plain(gated_normed, out_proj).astype(jnp.bfloat16)
    branch_other = lax.ppermute(branch, "tensor", swap)
    block_out = (
        input_f32 + (branch.astype(jnp.float32) + branch_other.astype(jnp.float32))
    ).astype(jnp.bfloat16)
    grad_out_proj = dot_inner(gated_normed, cotangent)
    grad_norm_gain = jnp.sum(d_gn * gated * gate_scale, axis=0)
    d_gated = gate_scale * weighted - gated * gate_scale**3 * gate_dot / INNER
    (
        d_conv_in,
        d_states,
        d_step_raw,
        d_gate_raw,
        grad_conv_value,
        grad_conv_value_bias,
        grad_step_bias,
        grad_decay_log,
        grad_skip_gain,
    ) = mixer_back(by_sequence(d_gated))
    d_bc_raw, grad_conv_state, grad_conv_state_bias = state_back(d_states)
    gate_bf = by_row(d_gate_raw).astype(jnp.bfloat16)
    value_bf = by_row(d_conv_in).astype(jnp.bfloat16)
    step_bf = by_row(d_step_raw).astype(jnp.bfloat16)
    state_bf = by_row(d_bc_raw).astype(jnp.bfloat16)
    head_terms = (
        dot_outer(gate_bf, gate_proj)
        + dot_outer(value_bf, value_proj)
        + dot_outer(step_bf, step_proj)
        + dot_outer(state_bf, state_proj)
    )
    grad_pre_gain = jnp.sum(head_terms * input_f32 * pre_scale, axis=0)
    mine = head_terms.astype(jnp.bfloat16)
    other = lax.ppermute(mine, "tensor", swap)
    d_normed = mine.astype(jnp.float32) + other.astype(jnp.float32)
    pre_dot = jnp.sum(d_normed * pre_gain[None, :] * input_f32, axis=1, keepdims=True)
    grad_input = (
        cotangent.astype(jnp.float32)
        + pre_scale * pre_gain[None, :] * d_normed
        - input_f32 * pre_scale**3 * pre_dot / D
    )

    def summed(array):
        return lax.psum(array.astype(jnp.bfloat16), "dp").astype(jnp.float32)

    grad_out_proj = summed(grad_out_proj)
    grad_gate_proj = summed(dot_inner(normed, gate_bf))
    grad_value_proj = summed(dot_inner(normed, value_bf))
    grad_step_proj = summed(dot_inner(normed, step_bf))
    grad_state_proj = lax.psum(
        dot_inner(normed, state_bf).astype(jnp.bfloat16), ("dp", "tensor")
    ).astype(jnp.float32)
    grad_pre_gain, grad_conv_state, grad_conv_state_bias = lax.psum(
        (grad_pre_gain, grad_conv_state, grad_conv_state_bias), ("dp", "tensor")
    )
    (
        grad_conv_value,
        grad_conv_value_bias,
        grad_step_bias,
        grad_decay_log,
        grad_skip_gain,
        grad_norm_gain,
    ) = lax.psum(
        (
            grad_conv_value,
            grad_conv_value_bias,
            grad_step_bias,
            grad_decay_log,
            grad_skip_gain,
            grad_norm_gain,
        ),
        "dp",
    )
    return (
        block_out,
        grad_input,
        grad_pre_gain,
        grad_gate_proj,
        grad_value_proj,
        grad_step_proj,
        grad_state_proj,
        grad_conv_value,
        grad_conv_value_bias,
        grad_conv_state,
        grad_conv_state_bias,
        grad_step_bias,
        grad_decay_log,
        grad_skip_gain,
        grad_norm_gain,
        grad_out_proj,
    )


def solution(mesh):
    placed = (
        P("dp", None),
        P("dp", None),
        P(),
        P(None, "tensor"),
        P(None, "tensor"),
        P(None, "tensor"),
        P(),
        P(None, "tensor"),
        P("tensor"),
        P(),
        P(),
        P("tensor"),
        P("tensor"),
        P("tensor"),
        P("tensor"),
        P("tensor", None),
    )
    return jax.shard_map(
        local,
        mesh=mesh,
        in_specs=placed,
        out_specs=(
            P("dp", None),
            P("dp", None),
            P(),
            P(None, "tensor"),
            P(None, "tensor"),
            P(None, "tensor"),
            P(),
            P(None, "tensor"),
            P("tensor"),
            P(),
            P(),
            P("tensor"),
            P("tensor"),
            P("tensor"),
            P("tensor"),
            P("tensor", None),
        ),
        check_vma=False,
    )
```
